512 devices in a mesh: dp: 32 (over z, core), mp: 16 (over x, y).
Axes of the slice: x: 4, y: 4, z: 16, core: 2. Of those that a mesh axis runs over, the one named last changes fastest.
Arguments:
- stream_in: bfloat16 [2048, 2048], P('dp', 'mp'), parts along dimension 0, may hold values from -24 to 24
- norm_gain: bfloat16 [2048], P('mp'), may hold values from 0.5 to 2
- gate_vals: bfloat16 [1024, 8192], P(None, 'mp'), may hold values from -0.1875 to 0.1875
- gate_mask: int32 [64, 8192], P(None, 'mp'), may hold values from 0 to 1679615
- up_vals: bfloat16 [1024, 8192], P(None, 'mp'), may hold values from -0.1875 to 0.1875
- up_mask: int32 [64, 8192], P(None, 'mp'), may hold values from 0 to 1679615
- down_vals: bfloat16 [4096, 2048], P('mp'), may hold values from -0.125 to 0.125
- down_mask: int32 [256, 2048], P('mp'), may hold values from 0 to 1679615
- final_gain: bfloat16 [2048], P('mp'), may hold values from 0.5 to 2
Outputs:
- stream_out: bfloat16 [2048, 2048], P('dp', 'mp'), parts along dimension 0
- final_normed: bfloat16 [2048, 2048], P('dp', 'mp'), parts along dimension 0
The draws below stay inside these ranges and needn't reach their ends.
There are 32 independent parts, one for each index of `dp`. The reference program is written for one: setup_inputs(seed, part) draws one part's arguments, and reference() takes and returns one part's arrays. A program takes and returns all parts, laid end to end along the dimension named above; an argument that names none is the same for every part. Nothing has to cross between parts.
Inputs may be any that keep to these rules, and one draw needn't show every extreme that they name: `gate_mask`: eight base-6 digits per entry, as the steps decode them. `up_mask`: eight base-6 digits per entry, as the steps decode them. `down_mask`: eight base-6 digits per entry, as the steps decode them.
All inputs are finite; a program needn't handle non-finite values.
Results may differ from the reference program's by a relative error of at most 0.017.
Values may be sent and summed in bfloat16 or wider, within the bound.
A program may use at most 64 MiB of HBM per device.

```python
import math
import jax
import jax.numpy as jnp
from jax import lax

D = 2048
FF = 8192
SEQS = 64
N_MP = 16


def draw_stream_in(key, part):
    row_key, col_key, body_key = jax.random.split(jax.random.fold_in(key, 11), 3)
    row_scale = jnp.exp(jax.random.uniform(row_key, (SEQS, 1), jnp.float32, jnp.log(0.05), jnp.log(0.5)))
    ramp = 1.0 + 2.0 * jnp.arange(D, dtype=jnp.float32)[None, :] / (D - 1)
    col_scale = ramp * jnp.exp(jax.random.uniform(col_key, (1, D), jnp.float32, jnp.log(0.4), jnp.log(4.0)))
    noise = jnp.clip(jax.random.normal(body_key, (SEQS, D), jnp.float32), -4.0, 4.0)
    values = row_scale * col_scale * noise
    return values.astype(jnp.bfloat16)


def place_ends(entries, stream_key, least, top_value):
    extent = entries.shape
    index_at = [jax.random.randint(jax.random.fold_in(stream_key, axis), (), 0, extent[axis]) for axis in range(len(extent))]
    entries = entries.at[tuple(index_at)].set(least)
    longest = extent.index(max(extent))
    index_at[longest] = (index_at[longest] + 1) % extent[longest]
    return entries.at[tuple(index_at)].set(top_value)


def strengthened(entries, key, source, target, parts, factor):
    owner, partner = [(jnp.arange(entries.shape[dim]) // (entries.shape[dim] // parts)).reshape([-1 if axis == dim else 1 for axis in range(entries.ndim)]) for dim in (source, target)]
    chosen = jax.random.permutation(key, parts)[partner]
    strong = (owner == chosen) | (owner == (partner + parts // 2) % parts)
    return jnp.where(strong, factor * entries, entries)


def levels(stream_key, dims, shards, smallest, top_value):
    level = 1.0
    for position, parts in shards:
        heights = jax.random.uniform(jax.random.fold_in(jax.random.fold_in(stream_key, 6), position), (parts,), jnp.float32, smallest / len(shards), top_value / len(shards))
        level = level * jnp.repeat(jnp.exp(heights), dims[position] // parts).reshape((-1,) + (1,) * (len(dims) - 1 - position))
    return level


def gaussian(key, shape, spread, limit, cuts=(), kind=jnp.bfloat16):
    values = spread * jax.random.normal(key, shape, jnp.float32)
    if cuts:
        values = values * levels(key, shape, cuts, -0.22, 0.18)
    return jnp.clip(values, -limit, limit).astype(kind)


def noise_with(stream_key, dims, scale, limit, cuts, heavy, kind=jnp.bfloat16):
    entries = scale * jax.random.normal(stream_key, dims, jnp.float32)
    if cuts:
        entries = entries * levels(stream_key, dims, cuts, -0.22, 0.18)
    return jnp.clip(strengthened(entries, jax.random.fold_in(stream_key, 3), *heavy), -limit, limit).astype(kind)


def setup_inputs(seed: int = 0, part: int = 0) -> dict:
    key_list = jax.random.split(jax.random.key(seed), 10)
    own_keys = jax.random.split(jax.random.fold_in(key_list[9], part), 10)
    stream_in = draw_stream_in(jax.random.fold_in(jax.random.fold_in(key_list[9], part), 71), part)
    norm_gain = jnp.clip(jnp.exp(math.log(2.0) - 1.3862944 * jax.random.uniform(key_list[1], (D,), jnp.float32) ** levels(key_list[1], (D,), ((0, 16),), -0.2, 0.2)), 0.5, 2.0).astype(jnp.bfloat16)
    gate_vals = gaussian(key_list[2], (D // 2, FF), (D // 2) ** -0.5, 0.1875, ((1, 16),))
    gate_mask = place_ends(jax.random.randint(key_list[3], (D // 32, FF), 0, 1679616), jax.random.fold_in(key_list[3], 1), 0, 1679615).astype(jnp.int32)
    up_vals = gaussian(key_list[4], (D // 2, FF), (D // 2) ** -0.5, 0.1875, ((1, 16),))
    up_mask = place_ends(jax.random.randint(key_list[5], (D // 32, FF), 0, 1679616), jax.random.fold_in(key_list[5], 1), 0, 1679615).astype(jnp.int32)
    down_vals = noise_with(key_list[6], (FF // 2, D), (FF // 2) ** -0.5, 0.125, ((0, 16),), (0, 1, 16, 2.0))
    down_mask = place_ends(jax.random.randint(key_list[7], (FF // 32, D), 0, 1679616), jax.random.fold_in(key_list[7], 1), 0, 1679615).astype(jnp.int32)
    final_gain = jnp.clip(jnp.exp(math.log(2.0) - 1.3862944 * jax.random.uniform(key_list[8], (D,), jnp.float32) ** levels(key_list[8], (D,), ((0, 16),), -0.2, 0.2)), 0.5, 2.0).astype(jnp.bfloat16)
    return {"stream_in": stream_in, "norm_gain": norm_gain, "gate_vals": gate_vals, "gate_mask": gate_mask, "up_vals": up_vals, "up_mask": up_mask, "down_vals": down_vals, "down_mask": down_mask, "final_gain": final_gain}


epsilon = 1e-05

def expand(values, packed):
    powers = jnp.array([6 ** digit_index for digit_index in range(8)], jnp.int32)
    digits = (packed[:, None, :] // powers[None, :, None] % 6).reshape(packed.shape[0] * 8, packed.shape[1])
    paired = values.reshape(digits.shape[0], 2, values.shape[1])
    first_val = paired[:, 0, :]
    second_val = paired[:, 1, :]
    zero_val = jnp.zeros((), values.dtype)
    row_zero = jnp.where(digits < 3, first_val, zero_val)
    row_one = jnp.where(digits == 0, second_val, jnp.where((digits == 3) | (digits == 4), first_val, zero_val))
    row_two = jnp.where(digits == 5, first_val, jnp.where((digits == 1) | (digits == 3), second_val, zero_val))
    row_three = jnp.where((digits == 2) | (digits >= 4), second_val, zero_val)
    dense = jnp.stack([row_zero, row_one, row_two, row_three], axis=1)
    return dense.reshape(digits.shape[0] * 4, values.shape[1])

def reference(stream_in, norm_gain, gate_vals, gate_mask, up_vals, up_mask, down_vals, down_mask, final_gain):
    stream_f = stream_in.astype(jnp.float32)
    mean_sq = lax.optimization_barrier(jnp.mean(stream_f * stream_f, axis=1, keepdims=True))
    normed = (stream_f * lax.rsqrt(mean_sq + epsilon) * norm_gain.astype(jnp.float32)).astype(jnp.bfloat16)
    gate_w = expand(gate_vals, gate_mask)
    up_w = expand(up_vals, up_mask)
    down_w = expand(down_vals, down_mask)
    gate_part = jnp.dot(normed, gate_w, preferred_element_type=jnp.float32)
    up_part = jnp.dot(normed, up_w, preferred_element_type=jnp.float32)
    hidden = (jax.nn.silu(gate_part) * up_part).astype(jnp.bfloat16)
    blocks = hidden.reshape(SEQS, N_MP, FF // N_MP).astype(jnp.float32)
    down_blocks = down_w.reshape(N_MP, FF // N_MP, D).astype(jnp.float32)
    partials = jnp.einsum('bkf,kfd->kbd', blocks, down_blocks).astype(jnp.bfloat16)
    total = lax.optimization_barrier(jnp.sum(partials.astype(jnp.float32), axis=0))
    stream_out = (stream_f + total).astype(jnp.bfloat16)
    out_f = stream_out.astype(jnp.float32)
    final_sq = lax.optimization_barrier(jnp.mean(out_f * out_f, axis=1, keepdims=True))
    final_normed = (out_f * lax.rsqrt(final_sq + epsilon) * final_gain.astype(jnp.float32)).astype(jnp.bfloat16)
    return (stream_out, final_normed)
```

```python
import functools

import jax
import jax.numpy as jnp
from jax import lax
from jax.experimental import pallas as pl
from jax.experimental.pallas import tpu as pltpu
from jax.sharding import PartitionSpec as P

MESH = pl.DeviceIdType.MESH
F32 = jnp.float32
BF16 = jnp.bfloat16
epsilon = 1e-05


def iota(shape, dim):
    return lax.broadcasted_iota(jnp.int32, shape, dim)


def decode_rows(vals, mask, width):
    row = iota((16, 1), 0)
    digit = row // 2
    odd = row % 2 == 1
    scale = jnp.zeros((16, 1), F32)
    for k in range(8):
        scale = jnp.where(digit == k, F32(1.0 / 6 ** (k + 1)), scale)
    scale = jnp.broadcast_to(scale, (16, 128))
    odd = jnp.broadcast_to(odd, (16, 128))
    first_top = jnp.where(odd, F32(1), F32(3))
    second_low = jnp.where(odd, F32(4), F32(5))
    middle = jnp.where(odd, F32(2.5), F32(100))
    zero = jnp.zeros((16, 128), F32)
    uppers, lowers = [], []
    for c in range(width // 128):
        lanes = slice(c * 128, c * 128 + 128)
        packed = jnp.broadcast_to(mask[:, lanes], (16, 128))
        turn = packed * scale
        place = (turn - jnp.floor(turn)) * F32(6)
        kept = vals[:, lanes].astype(F32)
        in_upper = place < first_top
        in_lower = (place > second_low) | (jnp.abs(place - middle) < F32(0.5))
        upper = jnp.where(in_upper, kept, zero)
        lower = jnp.where(in_lower, kept, zero)
        crossing = jnp.where(in_upper | in_lower, zero, kept)
        down = jnp.concatenate(
            [pltpu.roll(crossing[:8], 1, 0), pltpu.roll(crossing[8:], 1, 0)], axis=0
        )
        up = jnp.concatenate(
            [pltpu.roll(crossing[:8], 7, 0), pltpu.roll(crossing[8:], 7, 0)], axis=0
        )
        upper = jnp.where(odd, upper + down, upper)
        lower = jnp.where(odd, lower, lower + up)
        uppers.append(upper.astype(BF16))
        lowers.append(lower.astype(BF16))
    return jnp.concatenate(uppers, axis=1), jnp.concatenate(lowers, axis=1)


def permutation():
    source, target = iota((128, 128), 0), iota((128, 128), 1)
    q = target % 32
    order = target // 32 * 32 + (q % 16) // 2 * 4 + q % 2 + q // 16 * 2
    return jnp.where(source == order, F32(1), F32(0)).astype(BF16)


def row_sums_tile(values, eye):
    sums = jnp.sum(values, axis=1, keepdims=True)
    spread = jnp.where(eye, sums, F32(0))
    tile = spread[0:8]
    for v in range(1, 8):
        tile = tile + spread[8 * v : 8 * v + 8]
    return tile


def row_column(tile, eye):
    spread = jnp.where(eye, jnp.concatenate([tile] * 8, axis=0), F32(0))
    return jnp.sum(spread, axis=1, keepdims=True)


def kernel(
    n,
    ny,
    x_ref,
    ngain_ref,
    fgain_ref,
    gv_hbm,
    gm_hbm,
    uv_hbm,
    um_hbm,
    dv_hbm,
    dm_hbm,
    so_ref,
    fn_ref,
    gv,
    uv,
    dv,
    gm,
    um,
    dm,
    wgu,
    wd,
    acc,
    xbuf,
    part,
    rbuf,
    sbuf,
    load_sem,
    xs_sem,
    xr_sem,
    ps_sem,
    pr_sem,
    ss_sem,
    sr_sem,
):
    me = lax.axis_index("mp")
    nx = n // ny
    mx, my = me // ny, me % ny
    barrier = pltpu.get_barrier_semaphore()
    for step in range(1, n):
        peer = lax.rem(me + step, n)
        pl.semaphore_signal(barrier, inc=1, device_id={"mp": peer}, device_id_type=MESH)
    loads = [
        pltpu.make_async_copy(src, dst, load_sem.at[i])
        for i, (src, dst) in enumerate(
            [(gm_hbm, gm), (gv_hbm, gv), (um_hbm, um), (uv_hbm, uv), (dm_hbm, dm), (dv_hbm, dv)]
        )
    ]
    for load in loads:
        load.start()

    eye = iota((64, 128), 0) == iota((64, 128), 1)
    perm = permutation()
    x = x_ref[...].astype(F32)
    gained = (x * ngain_ref[...].astype(F32)).astype(BF16)
    gained = jnp.dot(gained, perm, preferred_element_type=F32).astype(BF16)
    tile = row_sums_tile(x * x, eye)
    high = tile.astype(BF16)
    rest = (tile - high.astype(F32)).astype(BF16)
    xbuf[me, 0:64, :] = gained
    xbuf[me, 64:80, :] = jnp.concatenate([high, rest], axis=0)

    pairs = []
    for dx in [2, 1, 3, 0]:
        for dy in [1, 0]:
            pairs.append(lax.rem(mx + dx, nx) * 2 + lax.rem(my // 2 + dy, 2))
    peers = []
    for pair in pairs[:-1]:
        peers += [2 * pair, 2 * pair + 1]
    peers.append(me + 1 - 2 * lax.rem(me, 2))

    def copies(src, dst, send, recv):
        out = []
        for peer in peers:
            out.append(
                (
                    pltpu.make_async_remote_copy(
                        src_ref=src(peer),
                        dst_ref=dst.at[me],
                        send_sem=send.at[peer],
                        recv_sem=recv.at[me],
                        device_id={"mp": peer},
                        device_id_type=MESH,
                    )
                )
            )
        return out

    def arrival(peer, dst, send, recv):
        return pltpu.make_async_remote_copy(
            src_ref=dst.at[peer],
            dst_ref=dst.at[peer],
            send_sem=send.at[peer],
            recv_sem=recv.at[peer],
            device_id={"mp": peer},
            device_id_type=MESH,
        )

    pl.semaphore_wait(barrier, n - 1)
    x_sends = copies(lambda peer: xbuf.at[me], xbuf, xs_sem, xr_sem)
    for send in x_sends:
        send.start()

    def decode_gate_up(vals, mask, at):
        def body(i, carry):
            row = mask[pl.ds(i, 1), :].astype(F32) + F32(0.5)
            rows = vals[pl.ds(pl.multiple_of(i * 16, 16), 16), :]
            upper, lower = decode_rows(rows, row, 512)
            start = pl.multiple_of(i * 32, 32)
            wgu[pl.ds(start, 16), at : at + 512] = upper
            wgu[pl.ds(start + 16, 16), at : at + 512] = lower
            return carry

        lax.fori_loop(0, 64, body, 0)

    loads[0].wait()
    loads[1].wait()
    decode_gate_up(gv, gm, 0)
    loads[2].wait()
    loads[3].wait()
    decode_gate_up(uv, um, 512)
    loads[4].wait()
    loads[5].wait()

    def decode_down(i, carry):
        for c in range(4):
            lanes = slice(c * 512, c * 512 + 512)
            row = dm[pl.ds(i, 1), lanes].astype(F32) + F32(0.5)
            rows = dv[pl.ds(pl.multiple_of(i * 16, 16), 16), lanes]
            upper, lower = decode_rows(rows, row, 512)
            start = pl.multiple_of(i * 32, 32)
            wd[pl.ds(start, 16), lanes] = upper
            wd[pl.ds(start + 16, 16), lanes] = lower
        return carry

    lax.fori_loop(0, 16, decode_down, 0)

    total = None
    for index, pair in enumerate(pairs[::-1]):
        if index == 0:
            arrival(peers[-1], xbuf, xs_sem, xr_sem).wait_recv()
        else:
            arrival(2 * pair, xbuf, xs_sem, xr_sem).wait_recv()
            arrival(2 * pair + 1, xbuf, xs_sem, xr_sem).wait_recv()
        left, right = xbuf[2 * pair], xbuf[2 * pair + 1]
        block = jnp.concatenate([left[0:64], right[0:64]], axis=1)
        for side in (left, right):
            tile = side[64:72].astype(F32) + side[72:80].astype(F32)
            total = tile if total is None else total + tile
        depth = pl.ds(pl.multiple_of(pair * 256, 256), 256)
        for c in range(2):
            lanes = slice(c * 512, c * 512 + 512)
            product = jnp.dot(block, wgu[depth, lanes], preferred_element_type=F32)
            if index == 0:
                acc[:, lanes] = product
            else:
                acc[:, lanes] += product

    scale = lax.rsqrt(row_column(total, eye) / F32(n * 128) + F32(epsilon))
    gate = acc[:, 0:512] * scale
    up = acc[:, 512:1024] * scale
    hidden = (jax.nn.silu(gate) * up).astype(BF16)
    hidden = jnp.concatenate(
        [
            jnp.dot(hidden[:, c * 128 : c * 128 + 128], perm, preferred_element_type=F32)
            for c in range(4)
        ],
        axis=1,
    ).astype(BF16)

    p_sends = copies(lambda peer: part.at[peer], rbuf, ps_sem, pr_sem)
    for index, pair in enumerate(pairs):
        lanes = pl.ds(pl.multiple_of(pair * 256, 256), 256)
        product = jnp.dot(hidden, wd[:, lanes], preferred_element_type=F32).astype(BF16)
        part[2 * pair] = product[:, 0:128]
        part[2 * pair + 1] = product[:, 128:256]
        for send in p_sends[2 * index : 2 * index + 2]:
            send.start()

    summed = part[me].astype(F32)
    for peer in peers[::-1]:
        arrival(peer, rbuf, ps_sem, pr_sem).wait_recv()
        summed += rbuf[peer].astype(F32)
    out = (x_ref[...].astype(F32) + summed).astype(BF16)
    so_ref[...] = out
    out = out.astype(F32)
    sbuf[me] = row_sums_tile(out * out, eye)
    s_sends = copies(lambda peer: sbuf.at[me], sbuf, ss_sem, sr_sem)
    for send in s_sends:
        send.start()
    total = sbuf[me]
    for peer in peers[::-1]:
        arrival(peer, sbuf, ss_sem, sr_sem).wait_recv()
        total += sbuf[peer]
    scale = lax.rsqrt(row_column(total, eye) / F32(n * 128) + F32(epsilon))
    fn_ref[...] = (out * scale * fgain_ref[...].astype(F32)).astype(BF16)
    for send in x_sends + p_sends + s_sends:
        send.wait_send()


def solution(mesh):
    n = mesh.shape["mp"]
    vmem = pl.BlockSpec(memory_space=pltpu.VMEM)
    hbm = pl.BlockSpec(memory_space=pl.ANY)

    def step(stream, ngain, gv, gm, uv, um, dv, dm, fgain):
        block = jax.ShapeDtypeStruct(stream.shape, BF16)
        dma = pltpu.SemaphoreType.DMA
        return pl.pallas_call(
            functools.partial(kernel, n, 4),
            out_shape=(block, block),
            in_specs=[vmem] * 3 + [hbm] * 6,
            out_specs=(vmem, vmem),
            scratch_shapes=[
                pltpu.VMEM(gv.shape, BF16),
                pltpu.VMEM(uv.shape, BF16),
                pltpu.VMEM(dv.shape, BF16),
                pltpu.VMEM(gm.shape, jnp.int32),
                pltpu.VMEM(um.shape, jnp.int32),
                pltpu.VMEM(dm.shape, jnp.int32),
                pltpu.VMEM((2048, 1024), BF16),
                pltpu.VMEM((512, 2048), BF16),
                pltpu.VMEM((64, 1024), F32),
                pltpu.VMEM((n, 80, 128), BF16),
                pltpu.VMEM((n, 64, 128), BF16),
                pltpu.VMEM((n, 64, 128), BF16),
                pltpu.VMEM((n, 8, 128), F32),
                dma((6,)),
                dma((n,)),
                dma((n,)),
                dma((n,)),
                dma((n,)),
                dma((n,)),
                dma((n,)),
            ],
            compiler_params=pltpu.CompilerParams(collective_id=0, has_side_effects=True),
        )(stream, ngain.reshape(1, -1), fgain.reshape(1, -1), gv, gm, uv, um, dv, dm)

    cols = P(None, "mp")
    return jax.shard_map(
        step,
        mesh=mesh,
        in_specs=(
            P("dp", "mp"),
            P("mp"),
            cols,
            cols,
            cols,
            cols,
            P("mp", None),
            P("mp", None),
            P("mp"),
        ),
        out_specs=(P("dp", "mp"), P("dp", "mp")),
        check_vma=False,
    )
```

```python
import functools

import jax
import jax.numpy as jnp
from jax import lax
from jax.experimental import pallas as pl
from jax.experimental.pallas import tpu as pltpu
from jax.sharding import PartitionSpec as P

MESH = pl.DeviceIdType.MESH
F32 = jnp.float32
BF16 = jnp.bfloat16
epsilon = 1e-05


def iota(shape, dim):
    return lax.broadcasted_iota(jnp.int32, shape, dim)


def decode_rows(vals, mask, width):
    row = iota((16, 1), 0)
    digit = row // 2
    odd = row % 2 == 1
    scale = jnp.zeros((16, 1), F32)
    for k in range(8):
        scale = jnp.where(digit == k, F32(1.0 / 6 ** (k + 1)), scale)
    scale = jnp.broadcast_to(scale, (16, 128))
    odd = jnp.broadcast_to(odd, (16, 128))
    first_top = jnp.where(odd, F32(1), F32(3))
    second_low = jnp.where(odd, F32(4), F32(5))
    middle = jnp.where(odd, F32(2.5), F32(100))
    zero = jnp.zeros((16, 128), F32)
    uppers, lowers = [], []
    for c in range(width // 128):
        lanes = slice(c * 128, c * 128 + 128)
        packed = jnp.broadcast_to(mask[:, lanes], (16, 128))
        turn = packed * scale
        place = (turn - jnp.floor(turn)) * F32(6)
        kept = vals[:, lanes].astype(F32)
        in_upper = place < first_top
        in_lower = (place > second_low) | (jnp.abs(place - middle) < F32(0.5))
        upper = jnp.where(in_upper, kept, zero)
        lower = jnp.where(in_lower, kept, zero)
        crossing = jnp.where(in_upper | in_lower, zero, kept)
        down = jnp.concatenate(
            [pltpu.roll(crossing[:8], 1, 0), pltpu.roll(crossing[8:], 1, 0)], axis=0
        )
        up = jnp.concatenate(
            [pltpu.roll(crossing[:8], 7, 0), pltpu.roll(crossing[8:], 7, 0)], axis=0
        )
        upper = jnp.where(odd, upper + down, upper)
        lower = jnp.where(odd, lower, lower + up)
        uppers.append(upper.astype(BF16))
        lowers.append(lower.astype(BF16))
    return jnp.concatenate(uppers, axis=1), jnp.concatenate(lowers, axis=1)


def permutation():
    source, target = iota((128, 128), 0), iota((128, 128), 1)
    q = target % 32
    order = target // 32 * 32 + (q % 16) // 2 * 4 + q % 2 + q // 16 * 2
    return jnp.where(source == order, F32(1), F32(0)).astype(BF16)


def row_sums(values, eye):
    sums = jnp.sum(values, axis=1, keepdims=True)
    return jnp.sum(jnp.where(eye, sums, F32(0)), axis=0, keepdims=True)


def row_column(rows, eye):
    total = jnp.sum(rows[:, 0, :], axis=0, keepdims=True)
    return jnp.sum(jnp.where(eye, total, F32(0)), axis=1, keepdims=True)


def kernel(
    n,
    ny,
    x_hbm,
    ngain_hbm,
    fgain_hbm,
    gv_hbm,
    gm_hbm,
    uv_hbm,
    um_hbm,
    dv_hbm,
    dm_hbm,
    so_ref,
    fn_ref,
    x_ref,
    ngain_ref,
    fgain_ref,
    gv,
    uv,
    dv,
    gm,
    um,
    dm,
    wgu,
    wd,
    acc,
    xbuf,
    qbuf,
    part,
    rbuf,
    sbuf,
    load_sem,
    xs_sem,
    xr_sem,
    qs_sem,
    qr_sem,
    ps_sem,
    pr_sem,
    ss_sem,
    sr_sem,
):
    me = lax.axis_index("mp")
    nx = n // ny
    mx, my = me // ny, me % ny
    barrier = pltpu.get_barrier_semaphore()
    for step in range(1, n):
        peer = lax.rem(me + step, n)
        pl.semaphore_signal(barrier, inc=1, device_id={"mp": peer}, device_id_type=MESH)
    loads = [
        pltpu.make_async_copy(src, dst, load_sem.at[i])
        for i, (src, dst) in enumerate(
            [
                (x_hbm, x_ref),
                (ngain_hbm, ngain_ref),
                (fgain_hbm, fgain_ref),
                (gm_hbm, gm), (gv_hbm, gv),
                (um_hbm, um),
                (uv_hbm, uv),
                (dm_hbm, dm),
                (dv_hbm, dv),
            ]
        )
    ]
    for load in loads:
        load.start()

    eye = iota((64, 128), 0) == iota((64, 128), 1)
    perm = permutation()
    for load in loads[:3]:
        load.wait()
    x = x_ref[...].astype(F32)
    gained = (x * ngain_ref[...].astype(F32)).astype(BF16)
    xbuf[me] = jnp.dot(gained, perm, preferred_element_type=F32).astype(BF16)
    qbuf[me] = row_sums(x * x, eye)

    pairs = []
    for dx in [2, 1, 3, 0]:
        for dy in [1, 0]:
            pairs.append(lax.rem(mx + dx, nx) * 2 + lax.rem(my // 2 + dy, 2))
    peers = []
    for pair in pairs[:-1]:
        peers += [2 * pair, 2 * pair + 1]
    peers.append(me + 1 - 2 * lax.rem(me, 2))

    def copies(src, dst, send, recv):
        out = []
        for peer in peers:
            out.append(
                (
                    pltpu.make_async_remote_copy(
                        src_ref=src(peer),
                        dst_ref=dst.at[me],
                        send_sem=send.at[peer],
                        recv_sem=recv.at[me],
                        device_id={"mp": peer},
                        device_id_type=MESH,
                    )
                )
            )
        return out

    def arrival(peer, dst, send, recv):
        return pltpu.make_async_remote_copy(
            src_ref=dst.at[peer],
            dst_ref=dst.at[peer],
            send_sem=send.at[peer],
            recv_sem=recv.at[peer],
            device_id={"mp": peer},
            device_id_type=MESH,
        )

    pl.semaphore_wait(barrier, n - 1)
    x_sends = copies(lambda peer: xbuf.at[me], xbuf, xs_sem, xr_sem)
    q_sends = copies(lambda peer: qbuf.at[me], qbuf, qs_sem, qr_sem)
    for send in x_sends + q_sends:
        send.start()

    def decode_gate_up(vals, mask, at):
        def body(i, carry):
            row = mask[pl.ds(i, 1), :].astype(F32) + F32(0.5)
            rows = vals[pl.ds(pl.multiple_of(i * 16, 16), 16), :]
            upper, lower = decode_rows(rows, row, 512)
            start = pl.multiple_of(i * 32, 32)
            wgu[pl.ds(start, 16), at : at + 512] = upper
            wgu[pl.ds(start + 16, 16), at : at + 512] = lower
            return carry

        lax.fori_loop(0, 64, body, 0)

    loads[3].wait()
    loads[4].wait()
    decode_gate_up(gv, gm, 0)
    loads[5].wait()
    loads[6].wait()
    decode_gate_up(uv, um, 512)
    loads[7].wait()
    loads[8].wait()

    def decode_down(i, carry):
        for c in range(4):
            lanes = slice(c * 512, c * 512 + 512)
            row = dm[pl.ds(i, 1), lanes].astype(F32) + F32(0.5)
            rows = dv[pl.ds(pl.multiple_of(i * 16, 16), 16), lanes]
            upper, lower = decode_rows(rows, row, 512)
            start = pl.multiple_of(i * 32, 32)
            wd[pl.ds(start, 16), lanes] = upper
            wd[pl.ds(start + 16, 16), lanes] = lower
        return carry

    lax.fori_loop(0, 16, decode_down, 0)

    for index, pair in enumerate(pairs[::-1]):
        if index == 0:
            arrival(peers[-1], xbuf, xs_sem, xr_sem).wait_recv()
        else:
            arrival(2 * pair, xbuf, xs_sem, xr_sem).wait_recv()
            arrival(2 * pair + 1, xbuf, xs_sem, xr_sem).wait_recv()
        block = jnp.concatenate([xbuf[2 * pair], xbuf[2 * pair + 1]], axis=1)
        depth = pl.ds(pl.multiple_of(pair * 256, 256), 256)
        for c in range(2):
            lanes = slice(c * 512, c * 512 + 512)
            product = jnp.dot(block, wgu[depth, lanes], preferred_element_type=F32)
            if index == 0:
                acc[:, lanes] = product
            else:
                acc[:, lanes] += product

    for peer in peers[::-1]:
        arrival(peer, qbuf, qs_sem, qr_sem).wait_recv()
    scale = lax.rsqrt(row_column(qbuf[...], eye) / F32(n * 128) + F32(epsilon))
    gate = acc[:, 0:512] * scale
    up = acc[:, 512:1024] * scale
    hidden = (jax.nn.silu(gate) * up).astype(BF16)
    hidden = jnp.concatenate(
        [
            jnp.dot(hidden[:, c * 128 : c * 128 + 128], perm, preferred_element_type=F32)
            for c in range(4)
        ],
        axis=1,
    ).astype(BF16)

    p_sends = copies(lambda peer: part.at[peer], rbuf, ps_sem, pr_sem)
    for index, pair in enumerate(pairs):
        lanes = pl.ds(pl.multiple_of(pair * 256, 256), 256)
        product = jnp.dot(hidden, wd[:, lanes], preferred_element_type=F32).astype(BF16)
        part[2 * pair] = product[:, 0:128]
        part[2 * pair + 1] = product[:, 128:256]
        for send in p_sends[2 * index : 2 * index + 2]:
            send.start()

    summed = part[me].astype(F32)
    for peer in peers[::-1]:
        arrival(peer, rbuf, ps_sem, pr_sem).wait_recv()
        summed += rbuf[peer].astype(F32)
    out = (x_ref[...].astype(F32) + summed).astype(BF16)
    out = out.astype(F32)
    so_ref[...] = out
    sbuf[me] = row_sums(out * out, eye)
    s_sends = copies(lambda peer: sbuf.at[me], sbuf, ss_sem, sr_sem)
    for send in s_sends:
        send.start()
    for peer in peers[::-1]:
        arrival(peer, sbuf, ss_sem, sr_sem).wait_recv()
    scale = lax.rsqrt(row_column(sbuf[...], eye) / F32(n * 128) + F32(epsilon))
    fn_ref[...] = scale * fgain_ref[...].astype(F32)
    for send in x_sends + q_sends + p_sends + s_sends:
        send.wait_send()


def solution(mesh):
    n = mesh.shape["mp"]
    vmem = pl.BlockSpec(memory_space=pltpu.VMEM)
    hbm = pl.BlockSpec(memory_space=pl.ANY)

    def step(stream, ngain, gv, gm, uv, um, dv, dm, fgain):
        block = pltpu.VMEM(stream.shape, F32)
        dma = pltpu.SemaphoreType.DMA
        out, factor = pl.pallas_call(
            functools.partial(kernel, n, 4),
            out_shape=(block, block),
            in_specs=[hbm] * 9,
            out_specs=(vmem, vmem),
            scratch_shapes=[
                pltpu.VMEM(stream.shape, BF16),
                pltpu.VMEM((1, 128), BF16),
                pltpu.VMEM((1, 128), BF16),
                pltpu.VMEM(gv.shape, BF16),
                pltpu.VMEM(uv.shape, BF16),
                pltpu.VMEM(dv.shape, BF16),
                pltpu.VMEM(gm.shape, jnp.int32),
                pltpu.VMEM(um.shape, jnp.int32),
                pltpu.VMEM(dm.shape, jnp.int32),
                pltpu.VMEM((2048, 1024), BF16),
                pltpu.VMEM((512, 2048), BF16),
                pltpu.VMEM((64, 1024), F32),
                pltpu.VMEM((n, 64, 128), BF16),
                pltpu.VMEM((n, 1, 128), F32),
                pltpu.VMEM((n, 64, 128), BF16),
                pltpu.VMEM((n, 64, 128), BF16),
                pltpu.VMEM((n, 1, 128), F32),
                dma((9,)),
                dma((n,)),
                dma((n,)),
                dma((n,)),
                dma((n,)),
                dma((n,)),
                dma((n,)),
                dma((n,)),
                dma((n,)),
            ],
            compiler_params=pltpu.CompilerParams(collective_id=0, has_side_effects=True),
        )(stream, ngain.reshape(1, -1), fgain.reshape(1, -1), gv, gm, uv, um, dv, dm)
        return out.astype(BF16), (out * factor).astype(BF16)

    cols = P(None, "mp")
    return jax.shard_map(
        step,
        mesh=mesh,
        in_specs=(
            P("dp", "mp"),
            P("mp"),
            cols,
            cols,
            cols,
            cols,
            P("mp", None),
            P("mp", None),
            P("mp"),
        ),
        out_specs=(P("dp", "mp"), P("dp", "mp")),
        check_vma=False,
    )
```

```python
import functools

import jax
import jax.numpy as jnp
from jax import lax
from jax.experimental import pallas as pl
from jax.experimental.pallas import tpu as pltpu
from jax.sharding import PartitionSpec as P

MESH = pl.DeviceIdType.MESH
F32 = jnp.float32
BF16 = jnp.bfloat16
epsilon = 1e-05


def iota(shape, dim):
    return lax.broadcasted_iota(jnp.int32, shape, dim)


def sublanes(array, index):
    return jnp.take_along_axis(array, index, axis=0, mode="promise_in_bounds")


def decode_rows(vals, mask, width):
    group = iota((8, 128), 0)
    scale = jnp.zeros((8, 128), F32)
    for k in range(8):
        scale = jnp.where(group == k, F32(1.0 / 6 ** (k + 1)), scale)
    row = iota((16, 128), 0)
    odd = (row - row // 2 * 2).astype(F32).astype(BF16)
    second = odd > BF16(0.5)
    upper_top = BF16(3) - BF16(2) * odd
    lower_low = BF16(4.5) - odd
    lower_also = BF16(9) - BF16(7) * odd
    zero = jnp.zeros((16, 128), BF16)
    other = group + 1 - 2 * (group - group // 2 * 2)
    uppers, lowers = [], []
    for c in range(width // 128):
        lanes = slice(c * 128, c * 128 + 128)
        turn = jnp.broadcast_to(mask[:, lanes], (8, 128)) * scale
        digit = jnp.floor((turn - jnp.floor(turn)) * F32(6))
        digit = jnp.concatenate(
            [sublanes(digit, group // 2), sublanes(digit, group // 2 + 4)], axis=0
        ).astype(BF16)
        kept = vals[:, lanes]
        in_upper = digit < upper_top
        in_lower = (digit > lower_low) | (digit == lower_also)
        crossing = jnp.where(in_upper | in_lower, zero, kept).astype(F32)
        crossed = jnp.concatenate(
            [sublanes(crossing[:8], other), sublanes(crossing[8:], other)], axis=0
        ).astype(BF16)
        uppers.append(jnp.where(in_upper, kept, jnp.where(second, crossed, zero)))
        lowers.append(jnp.where(in_lower, kept, jnp.where(second, zero, crossed)))
    return jnp.concatenate(uppers, axis=1), jnp.concatenate(lowers, axis=1)


def column_order(shape):
    target = iota(shape, 1)
    q = target % 32
    return target // 32 * 32 + (q % 16) // 2 * 4 + q % 2 + q // 16 * 2


def row_sums(values, eye):
    sums = jnp.sum(values, axis=1, keepdims=True)
    return jnp.sum(jnp.where(eye, sums, F32(0)), axis=0, keepdims=True)


def row_column(row, eye):
    return jnp.sum(jnp.where(eye, row, F32(0)), axis=1, keepdims=True)


def kernel(
    n,
    ny,
    x_hbm,
    ngain_hbm,
    fgain_hbm,
    gv_hbm,
    gm_hbm,
    uv_hbm,
    um_hbm,
    dv_hbm,
    dm_hbm,
    so_ref,
    fn_ref,
    x_ref,
    ngain_ref,
    fgain_ref,
    gv,
    uv,
    dv,
    gm,
    um,
    dm,
    wgu,
    wd,
    acc,
    xbuf,
    part,
    rbuf,
    sbuf,
    load_sem,
    xs_sem,
    xr_sem,
    ps_sem,
    pr_sem,
    ss_sem,
    sr_sem,
):
    me = lax.axis_index("mp")
    nx = n // ny
    mx, my = me // ny, me % ny
    loads = [
        pltpu.make_async_copy(src, dst, load_sem.at[i])
        for i, src, dst in [
            (0, x_hbm, x_ref),
            (0, ngain_hbm, ngain_ref),
            (1, gm_hbm, gm),
            (1, gv_hbm, gv),
            (1, um_hbm, um),
            (1, uv_hbm, uv),
            (2, dm_hbm, dm),
            (2, dv_hbm, dv),
            (2, fgain_hbm, fgain_ref),
        ]
    ]
    for load in loads[:2]:
        load.start()
    barrier = pltpu.get_barrier_semaphore()
    peers = [
        lax.rem(mx + dx, nx) * ny + lax.rem(my + dy, ny)
        for dx, dy in [
            (2, 2), (2, 1), (1, 2), (2, 3), (3, 2), (1, 1), (1, 3), (3, 1),
            (3, 3), (2, 0), (0, 2), (1, 0), (3, 0), (0, 1), (0, 3),
        ]
    ]
    for peer in peers:
        pl.semaphore_signal(barrier, inc=1, device_id={"mp": peer}, device_id_type=MESH)
    for load in loads[2:]:
        load.start()

    eye = iota((64, 128), 0) == iota((64, 128), 1)
    order = column_order((64, 128))
    for load in loads[:2]:
        load.wait()
    x = x_ref[...].astype(F32)
    gained = x * ngain_ref[...].astype(F32)
    gained = jnp.take_along_axis(gained, order, axis=1, mode="promise_in_bounds")
    xbuf[me, 0:64, :] = gained.astype(BF16)
    sums = jnp.broadcast_to(row_sums(x * x, eye), (8, 128))
    high = sums.astype(BF16).astype(F32)
    xbuf[me, 64:72, :] = jnp.where(iota((8, 128), 0) == 0, high, sums - high).astype(BF16)

    def copies(src, dst, send, recv):
        return [
            pltpu.make_async_remote_copy(
                src_ref=src(peer),
                dst_ref=dst.at[me],
                send_sem=send,
                recv_sem=recv,
                device_id={"mp": peer},
                device_id_type=MESH,
            )
            for peer in peers
        ]

    def wait_bytes(ref, sem):
        pltpu.make_async_copy(ref, ref, sem).wait()

    pl.semaphore_wait(barrier, n - 1)
    x_sends = copies(lambda peer: xbuf.at[me], xbuf, xs_sem, xr_sem.at[me // 2])
    for send in x_sends:
        send.start()

    def decode_gate_up(vals, mask, at):
        def body(i, carry):
            row = mask[pl.ds(i, 1), :].astype(F32) + F32(0.5)
            rows = vals[pl.ds(pl.multiple_of(i * 16, 16), 16), :]
            upper, lower = decode_rows(rows, row, 512)
            start = pl.multiple_of(i * 32, 32)
            wgu[pl.ds(start, 16), at : at + 512] = upper
            wgu[pl.ds(start + 16, 16), at : at + 512] = lower
            return carry

        lax.fori_loop(0, 64, body, 0)

    for load in loads[2:6]:
        load.wait()
    decode_gate_up(gv, gm, 0)
    decode_gate_up(uv, um, 512)
    for load in loads[6:]:
        load.wait()

    def decode_down(i, carry):
        for c in range(4):
            lanes = slice(c * 512, c * 512 + 512)
            row = dm[pl.ds(i, 1), lanes].astype(F32) + F32(0.5)
            rows = dv[pl.ds(pl.multiple_of(i * 16, 16), 16), lanes]
            upper, lower = decode_rows(rows, row, 512)
            start = pl.multiple_of(i * 32, 32)
            wd[pl.ds(start, 16), lanes] = upper
            wd[pl.ds(start + 16, 16), lanes] = lower
        return carry

    lax.fori_loop(0, 16, decode_down, 0)

    sums = jnp.zeros((1, 128), F32)
    for index, (dx, dy) in enumerate(
        [(0, 0), (0, 1), (1, 0), (3, 0), (1, 1), (3, 1), (2, 0), (2, 1)]
    ):
        pair = lax.rem(mx + dx, nx) * (ny // 2) + lax.rem(my // 2 + dy, ny // 2)
        wait_bytes(xbuf.at[pl.ds(0, 1 if index == 0 else 2)], xr_sem.at[pair])
        left, right = xbuf[2 * pair], xbuf[2 * pair + 1]
        block = jnp.concatenate([left[0:64], right[0:64]], axis=1)
        sides = left[64:72].astype(F32) + right[64:72].astype(F32)
        sums += sides[0:1] + sides[1:2]
        depth = pl.ds(pl.multiple_of(pair * 256, 256), 256)
        for c in range(2):
            lanes = slice(c * 512, c * 512 + 512)
            product = jnp.dot(block, wgu[depth, lanes], preferred_element_type=F32)
            if index == 0:
                acc[:, lanes] = product
            else:
                acc[:, lanes] += product

    scale = lax.rsqrt(row_column(sums, eye) / F32(n * 128) + F32(epsilon))
    gate = acc[:, 0:512] * scale
    up = acc[:, 512:1024] * scale
    hidden = jax.nn.silu(gate) * up
    hidden = jnp.concatenate(
        [
            jnp.take_along_axis(
                hidden[:, c * 128 : c * 128 + 128], order, axis=1, mode="promise_in_bounds"
            )
            for c in range(4)
        ],
        axis=1,
    ).astype(BF16)

    p_sends = copies(lambda peer: part.at[peer], rbuf, ps_sem, pr_sem)

    def down(first, second):
        rows = [wd[:, pl.ds(pl.multiple_of(to * 128, 128), 128)] for to in (first, second)]
        return jnp.dot(hidden, jnp.concatenate(rows, axis=1), preferred_element_type=F32)

    owners = peers + [me]
    product = down(*owners[0:2])
    for at in range(0, n, 2):
        later = down(*owners[at + 2 : at + 4]) if at + 2 < n else None
        product = product.astype(BF16)
        part[owners[at]] = product[:, 0:128]
        part[owners[at + 1]] = product[:, 128:256]
        for send in p_sends[at : at + 2]:
            send.start()
        product = later

    wait_bytes(rbuf.at[0 : n - 1], pr_sem)
    summed = part[me].astype(F32)
    for peer in peers:
        summed += rbuf[peer].astype(F32)
    out = (x_ref[...].astype(F32) + summed).astype(BF16)
    out = out.astype(F32)
    so_ref[...] = out
    sbuf[me] = row_sums(out * out, eye)
    s_sends = copies(lambda peer: sbuf.at[me], sbuf, ss_sem, sr_sem)
    for send in s_sends:
        send.start()
    wait_bytes(sbuf.at[0 : n - 1], sr_sem)
    scale = lax.rsqrt(row_column(jnp.sum(sbuf[:, 0, :], axis=0, keepdims=True), eye) / F32(n * 128) + F32(epsilon))
    fn_ref[...] = scale * fgain_ref[...].astype(F32)
    for ref, sem in [(xbuf, xs_sem), (part, ps_sem), (sbuf, ss_sem)]:
        wait_bytes(ref.at[0 : n - 1], sem)


def solution(mesh):
    n = mesh.shape["mp"]
    vmem = pl.BlockSpec(memory_space=pltpu.VMEM)
    hbm = pl.BlockSpec(memory_space=pl.ANY)

    def step(stream, ngain, gv, gm, uv, um, dv, dm, fgain):
        block = pltpu.VMEM(stream.shape, F32)
        dma = pltpu.SemaphoreType.DMA
        out, factor = pl.pallas_call(
            functools.partial(kernel, n, 4),
            out_shape=(block, block),
            in_specs=[hbm] * 9,
            out_specs=(vmem, vmem),
            scratch_shapes=[
                pltpu.VMEM(stream.shape, BF16),
                pltpu.VMEM((1, 128), BF16),
                pltpu.VMEM((1, 128), BF16),
                pltpu.VMEM(gv.shape, BF16),
                pltpu.VMEM(uv.shape, BF16),
                pltpu.VMEM(dv.shape, BF16),
                pltpu.VMEM(gm.shape, jnp.int32),
                pltpu.VMEM(um.shape, jnp.int32),
                pltpu.VMEM(dm.shape, jnp.int32),
                pltpu.VMEM((2048, 1024), BF16),
                pltpu.VMEM((512, 2048), BF16),
                pltpu.VMEM((64, 1024), F32),
                pltpu.VMEM((n, 72, 128), BF16),
                pltpu.VMEM((n, 64, 128), BF16),
                pltpu.VMEM((n, 64, 128), BF16),
                pltpu.VMEM((n, 1, 128), F32),
                dma((3,)),
                dma,
                dma((n // 2,)),
                dma,
                dma,
                dma,
                dma,
            ],
            compiler_params=pltpu.CompilerParams(collective_id=0, has_side_effects=True),
        )(stream, ngain.reshape(1, -1), fgain.reshape(1, -1), gv, gm, uv, um, dv, dm)
        return out.astype(BF16), (out * factor).astype(BF16)

    cols = P(None, "mp")
    return jax.shard_map(
        step,
        mesh=mesh,
        in_specs=(
            P("dp", "mp"),
            P("mp"),
            cols,
            cols,
            cols,
            cols,
            P("mp", None),
            P("mp", None),
            P("mp"),
        ),
        out_specs=(P("dp", "mp"), P("dp", "mp")),
        check_vma=False,
    )
```

```python
import functools

import jax
import jax.numpy as jnp
from jax import lax
from jax.experimental import pallas as pl
from jax.experimental.pallas import tpu as pltpu
from jax.sharding import PartitionSpec as P

MESH = pl.DeviceIdType.MESH
F32 = jnp.float32
BF16 = jnp.bfloat16
epsilon = 1e-05


def iota(shape, dim):
    return lax.broadcasted_iota(jnp.int32, shape, dim)


def sublanes(array, index):
    return jnp.take_along_axis(array, index, axis=0, mode="promise_in_bounds")


def decode_rows(vals, mask, width):
    group = iota((8, 128), 0)
    scale = jnp.zeros((8, 128), F32)
    for k in range(8):
        scale = jnp.where(group == k, F32(1.0 / 6 ** (k + 1)), scale)
    row = iota((16, 128), 0)
    odd = (row - row // 2 * 2).astype(F32).astype(BF16)
    second = odd > BF16(0.5)
    upper_top = BF16(3) - BF16(2) * odd
    lower_low = BF16(4.5) - odd
    lower_also = BF16(9) - BF16(7) * odd
    zero = jnp.zeros((16, 128), BF16)
    other = group + 1 - 2 * (group - group // 2 * 2)
    uppers, lowers = [], []
    for c in range(width // 128):
        lanes = slice(c * 128, c * 128 + 128)
        turn = jnp.broadcast_to(mask[:, lanes], (8, 128)) * scale
        digit = jnp.floor((turn - jnp.floor(turn)) * F32(6))
        digit = jnp.concatenate(
            [sublanes(digit, group // 2), sublanes(digit, group // 2 + 4)], axis=0
        ).astype(BF16)
        kept = vals[:, lanes]
        in_upper = digit < upper_top
        in_lower = (digit > lower_low) | (digit == lower_also)
        crossing = jnp.where(in_upper | in_lower, zero, kept).astype(F32)
        crossed = jnp.concatenate(
            [sublanes(crossing[:8], other), sublanes(crossing[8:], other)], axis=0
        ).astype(BF16)
        uppers.append(jnp.where(in_upper, kept, jnp.where(second, crossed, zero)))
        lowers.append(jnp.where(in_lower, kept, jnp.where(second, zero, crossed)))
    return jnp.concatenate(uppers, axis=1), jnp.concatenate(lowers, axis=1)


def column_order(shape):
    target = iota(shape, 1)
    q = target % 32
    return target // 32 * 32 + (q % 16) // 2 * 4 + q % 2 + q // 16 * 2


def row_sums(values, eye):
    sums = jnp.sum(values, axis=1, keepdims=True)
    return jnp.sum(jnp.where(eye, sums, F32(0)), axis=0, keepdims=True)


def row_column(row, eye):
    return jnp.sum(jnp.where(eye, row, F32(0)), axis=1, keepdims=True)


def kernel(
    n,
    ny,
    x_hbm,
    ngain_hbm,
    fgain_hbm,
    gv_hbm,
    gm_hbm,
    uv_hbm,
    um_hbm,
    dv_hbm,
    dm_hbm,
    so_ref,
    fn_ref,
    x_ref,
    ngain_ref,
    fgain_ref,
    gv,
    uv,
    dv,
    gm,
    um,
    dm,
    wgu,
    wd,
    acc,
    xbuf,
    qbuf,
    part,
    rbuf,
    sbuf,
    load_sem,
    qs_sem,
    qr_sem,
    xs_sem,
    xr_sem,
    ps_sem,
    pr_sem,
    ss_sem,
    sr_sem,
):
    me = lax.axis_index("mp")
    nx = n // ny
    mx, my = me // ny, me % ny
    loads = [
        pltpu.make_async_copy(src, dst, load_sem.at[i])
        for i, src, dst in [
            (0, x_hbm, x_ref),
            (0, ngain_hbm, ngain_ref),
            (1, gm_hbm, gm),
            (1, gv_hbm, gv),
            (2, um_hbm, um),
            (2, uv_hbm, uv),
            (3, dm_hbm, dm),
            (3, dv_hbm, dv),
            (3, fgain_hbm, fgain_ref),
        ]
    ]
    for load in loads[:2]:
        load.start()
    barrier = pltpu.get_barrier_semaphore()
    peers = [
        lax.rem(mx + dx, nx) * ny + lax.rem(my + dy, ny)
        for dx, dy in [
            (2, 2), (2, 1), (1, 2), (2, 3), (3, 2), (1, 1), (1, 3), (3, 1),
            (3, 3), (2, 0), (0, 2), (1, 0), (3, 0), (0, 1), (0, 3),
        ]
    ]
    for peer in peers:
        pl.semaphore_signal(barrier, inc=1, device_id={"mp": peer}, device_id_type=MESH)
    for load in loads[2:]:
        load.start()

    eye = iota((64, 128), 0) == iota((64, 128), 1)
    order = column_order((64, 128))
    for load in loads[:2]:
        load.wait()
    x = x_ref[...].astype(F32)
    gained = x * ngain_ref[...].astype(F32)
    gained = jnp.take_along_axis(gained, order, axis=1, mode="promise_in_bounds")
    xbuf[me] = gained.astype(BF16)
    qbuf[me] = row_sums(x * x, eye)

    def copies(src, dst, send, recv):
        return [
            pltpu.make_async_remote_copy(
                src_ref=src(peer),
                dst_ref=dst.at[me],
                send_sem=send,
                recv_sem=recv,
                device_id={"mp": peer},
                device_id_type=MESH,
            )
            for peer in peers
        ]

    def wait_bytes(ref, sem):
        pltpu.make_async_copy(ref, ref, sem).wait()

    pl.semaphore_wait(barrier, n - 1)
    q_sends = copies(lambda peer: qbuf.at[me], qbuf, qs_sem, qr_sem)
    x_sends = copies(lambda peer: xbuf.at[me], xbuf, xs_sem, xr_sem.at[me // 2])
    for send in q_sends + x_sends:
        send.start()

    def decode_gate_up(vals, mask, at):
        def body(i, carry):
            row = mask[pl.ds(i, 1), :].astype(F32) + F32(0.5)
            rows = vals[pl.ds(pl.multiple_of(i * 16, 16), 16), :]
            upper, lower = decode_rows(rows, row, 512)
            start = pl.multiple_of(i * 32, 32)
            wgu[pl.ds(start, 16), at : at + 512] = upper
            wgu[pl.ds(start + 16, 16), at : at + 512] = lower
            return carry

        lax.fori_loop(0, 64, body, 0)

    for load in loads[2:4]:
        load.wait()
    decode_gate_up(gv, gm, 0)
    for load in loads[4:6]:
        load.wait()
    decode_gate_up(uv, um, 512)
    for load in loads[6:]:
        load.wait()

    def decode_down(i, carry):
        for c in range(4):
            lanes = slice(c * 512, c * 512 + 512)
            row = dm[pl.ds(i, 1), lanes].astype(F32) + F32(0.5)
            rows = dv[pl.ds(pl.multiple_of(i * 16, 16), 16), lanes]
            upper, lower = decode_rows(rows, row, 512)
            start = pl.multiple_of(i * 32, 32)
            wd[pl.ds(start, 16), lanes] = upper
            wd[pl.ds(start + 16, 16), lanes] = lower
        return carry

    lax.fori_loop(0, 16, decode_down, 0)

    for index, (dx, dy) in enumerate(
        [(0, 0), (0, 1), (1, 0), (3, 0), (1, 1), (3, 1), (2, 0), (2, 1)]
    ):
        pair = lax.rem(mx + dx, nx) * (ny // 2) + lax.rem(my // 2 + dy, ny // 2)
        wait_bytes(xbuf.at[pl.ds(0, 1 if index == 0 else 2)], xr_sem.at[pair])
        block = jnp.concatenate([xbuf[2 * pair], xbuf[2 * pair + 1]], axis=1)
        if index == 5:
            wait_bytes(qbuf.at[0 : n - 1], qr_sem)
            total = jnp.sum(qbuf[:, 0, :], axis=0, keepdims=True)
            scale = lax.rsqrt(row_column(total, eye) / F32(n * 128) + F32(epsilon))
        depth = pl.ds(pl.multiple_of(pair * 256, 256), 256)
        for c in range(2):
            lanes = slice(c * 512, c * 512 + 512)
            product = jnp.dot(block, wgu[depth, lanes], preferred_element_type=F32)
            if index == 0:
                acc[:, lanes] = product
            else:
                acc[:, lanes] += product

    gate = acc[:, 0:512] * scale
    up = acc[:, 512:1024] * scale
    hidden = jax.nn.silu(gate) * up
    hidden = jnp.concatenate(
        [
            jnp.take_along_axis(
                hidden[:, c * 128 : c * 128 + 128], order, axis=1, mode="promise_in_bounds"
            )
            for c in range(4)
        ],
        axis=1,
    ).astype(BF16)

    p_sends = copies(lambda peer: part.at[peer], rbuf, ps_sem, pr_sem)

    def down(first, second):
        rows = [wd[:, pl.ds(pl.multiple_of(to * 128, 128), 128)] for to in (first, second)]
        return jnp.dot(hidden, jnp.concatenate(rows, axis=1), preferred_element_type=F32)

    owners = peers + [me]
    product = down(*owners[0:2])
    for at in range(0, n, 2):
        later = down(*owners[at + 2 : at + 4]) if at + 2 < n else None
        product = product.astype(BF16)
        part[owners[at]] = product[:, 0:128]
        part[owners[at + 1]] = product[:, 128:256]
        for send in p_sends[at : at + 2]:
            send.start()
        product = later

    wait_bytes(rbuf.at[0 : n - 1], pr_sem)
    summed = part[me].astype(F32)
    for peer in peers:
        summed += rbuf[peer].astype(F32)
    out = (x_ref[...].astype(F32) + summed).astype(BF16)
    out = out.astype(F32)
    so_ref[...] = out
    sbuf[me] = row_sums(out * out, eye)
    s_sends = copies(lambda peer: sbuf.at[me], sbuf, ss_sem, sr_sem)
    for send in s_sends:
        send.start()
    wait_bytes(sbuf.at[0 : n - 1], sr_sem)
    scale = lax.rsqrt(row_column(jnp.sum(sbuf[:, 0, :], axis=0, keepdims=True), eye) / F32(n * 128) + F32(epsilon))
    fn_ref[...] = scale * fgain_ref[...].astype(F32)
    for ref, sem in [(qbuf, qs_sem), (xbuf, xs_sem), (part, ps_sem), (sbuf, ss_sem)]:
        wait_bytes(ref.at[0 : n - 1], sem)


def solution(mesh):
    n = mesh.shape["mp"]
    vmem = pl.BlockSpec(memory_space=pltpu.VMEM)
    hbm = pl.BlockSpec(memory_space=pl.ANY)

    def step(stream, ngain, gv, gm, uv, um, dv, dm, fgain):
        block = pltpu.VMEM(stream.shape, F32)
        dma = pltpu.SemaphoreType.DMA
        out, factor = pl.pallas_call(
            functools.partial(kernel, n, 4),
            out_shape=(block, block),
            in_specs=[hbm] * 9,
            out_specs=(vmem, vmem),
            scratch_shapes=[
                pltpu.VMEM(stream.shape, BF16),
                pltpu.VMEM((1, 128), BF16),
                pltpu.VMEM((1, 128), BF16),
                pltpu.VMEM(gv.shape, BF16),
                pltpu.VMEM(uv.shape, BF16),
                pltpu.VMEM(dv.shape, BF16),
                pltpu.VMEM(gm.shape, jnp.int32),
                pltpu.VMEM(um.shape, jnp.int32),
                pltpu.VMEM(dm.shape, jnp.int32),
                pltpu.VMEM((2048, 1024), BF16),
                pltpu.VMEM((512, 2048), BF16),
                pltpu.VMEM((64, 1024), F32),
                pltpu.VMEM((n, 64, 128), BF16),
                pltpu.VMEM((n, 1, 128), F32),
                pltpu.VMEM((n, 64, 128), BF16),
                pltpu.VMEM((n, 64, 128), BF16),
                pltpu.VMEM((n, 1, 128), F32),
                dma((4,)),
                dma,
                dma,
                dma,
                dma((n // 2,)),
                dma,
                dma,
                dma,
                dma,
            ],
            compiler_params=pltpu.CompilerParams(collective_id=0, has_side_effects=True),
        )(stream, ngain.reshape(1, -1), fgain.reshape(1, -1), gv, gm, uv, um, dv, dm)
        return out.astype(BF16), (out * factor).astype(BF16)

    cols = P(None, "mp")
    return jax.shard_map(
        step,
        mesh=mesh,
        in_specs=(
            P("dp", "mp"),
            P("mp"),
            cols,
            cols,
            cols,
            cols,
            P("mp", None),
            P("mp", None),
            P("mp"),
        ),
        out_specs=(P("dp", "mp"), P("dp", "mp")),
        check_vma=False,
    )
```

```python
import functools

import jax
import jax.numpy as jnp
from jax import lax
from jax.experimental import pallas as pl
from jax.experimental.pallas import tpu as pltpu
from jax.sharding import PartitionSpec as P

MESH = pl.DeviceIdType.MESH
F32 = jnp.float32
BF16 = jnp.bfloat16
epsilon = 1e-05


def iota(shape, dim):
    return lax.broadcasted_iota(jnp.int32, shape, dim)


def sublanes(array, index):
    return jnp.take_along_axis(array, index, axis=0, mode="promise_in_bounds")


def decode_rows(vals, mask, width):
    group = iota((8, 128), 0)
    scale = jnp.zeros((8, 128), F32)
    for k in range(8):
        scale = jnp.where(group == k, F32(1.0 / 6 ** (k + 1)), scale)
    row = iota((16, 128), 0)
    odd = (row - row // 2 * 2).astype(F32).astype(BF16)
    second = odd > BF16(0.5)
    upper_top = BF16(3) - BF16(2) * odd
    lower_low = BF16(4.5) - odd
    lower_also = BF16(9) - BF16(7) * odd
    zero = jnp.zeros((16, 128), BF16)
    other = group + 1 - 2 * (group - group // 2 * 2)
    uppers, lowers = [], []
    for c in range(width // 128):
        lanes = slice(c * 128, c * 128 + 128)
        turn = jnp.broadcast_to(mask[:, lanes], (8, 128)) * scale
        digit = jnp.floor((turn - jnp.floor(turn)) * F32(6))
        digit = jnp.concatenate(
            [sublanes(digit, group // 2), sublanes(digit, group // 2 + 4)], axis=0
        ).astype(BF16)
        kept = vals[:, lanes]
        in_upper = digit < upper_top
        in_lower = (digit > lower_low) | (digit == lower_also)
        crossing = jnp.where(in_upper | in_lower, zero, kept).astype(F32)
        crossed = jnp.concatenate(
            [sublanes(crossing[:8], other), sublanes(crossing[8:], other)], axis=0
        ).astype(BF16)
        uppers.append(jnp.where(in_upper, kept, jnp.where(second, crossed, zero)))
        lowers.append(jnp.where(in_lower, kept, jnp.where(second, zero, crossed)))
    return jnp.concatenate(uppers, axis=1), jnp.concatenate(lowers, axis=1)


def column_order(shape):
    target = iota(shape, 1)
    q = target % 32
    return target // 32 * 32 + (q % 16) // 2 * 4 + q % 2 + q // 16 * 2


def row_sums(values, eye):
    sums = jnp.sum(values, axis=1, keepdims=True)
    return jnp.sum(jnp.where(eye, sums, F32(0)), axis=0, keepdims=True)


def row_column(row, eye):
    return jnp.sum(jnp.where(eye, row, F32(0)), axis=1, keepdims=True)


def kernel(
    n,
    ny,
    x_hbm,
    ngain_hbm,
    fgain_hbm,
    gv_hbm,
    gm_hbm,
    uv_hbm,
    um_hbm,
    dv_hbm,
    dm_hbm,
    so_ref,
    fn_ref,
    x_ref,
    ngain_ref,
    fgain_ref,
    gv,
    uv,
    dv,
    gm,
    um,
    dm,
    wgu,
    wd,
    acc,
    xbuf,
    qbuf,
    part,
    rbuf,
    sbuf,
    load_sem,
    qs_sem,
    qr_sem,
    xs_sem,
    xr_sem,
    ps_sem,
    pr_sem,
    ss_sem,
    sr_sem,
):
    me = lax.axis_index("mp")
    nx = n // ny
    mx, my = me // ny, me % ny
    loads = [
        pltpu.make_async_copy(src, dst, load_sem.at[i])
        for i, src, dst in [
            (0, x_hbm, x_ref),
            (0, ngain_hbm, ngain_ref),
            (1, gm_hbm, gm),
            (1, gv_hbm, gv),
            (2, um_hbm, um),
            (2, uv_hbm, uv),
            (2, dm_hbm, dm),
            (2, dv_hbm, dv),
            (2, fgain_hbm, fgain_ref),
        ]
    ]
    for load in loads[:2]:
        load.start()
    barrier = pltpu.get_barrier_semaphore()
    peers = [
        lax.rem(mx + dx, nx) * ny + lax.rem(my + dy, ny)
        for dx, dy in [
            (2, 2), (2, 1), (1, 2), (2, 3), (3, 2), (1, 1), (1, 3), (3, 1),
            (3, 3), (2, 0), (0, 2), (1, 0), (3, 0), (0, 1), (0, 3),
        ]
    ]
    for peer in peers:
        pl.semaphore_signal(barrier, inc=1, device_id={"mp": peer}, device_id_type=MESH)
    for load in loads[2:]:
        load.start()

    eye = iota((64, 128), 0) == iota((64, 128), 1)
    order = column_order((64, 128))
    for load in loads[:2]:
        load.wait()
    x = x_ref[...].astype(F32)
    gained = x * ngain_ref[...].astype(F32)
    gained = jnp.take_along_axis(gained, order, axis=1, mode="promise_in_bounds")
    xbuf[me] = gained.astype(BF16)
    qbuf[me] = row_sums(x * x, eye)

    def copies(src, dst, send, recv):
        return [
            pltpu.make_async_remote_copy(
                src_ref=src(peer),
                dst_ref=dst.at[me],
                send_sem=send,
                recv_sem=recv,
                device_id={"mp": peer},
                device_id_type=MESH,
            )
            for peer in peers
        ]

    def wait_bytes(ref, sem):
        pltpu.make_async_copy(ref, ref, sem).wait()

    pl.semaphore_wait(barrier, n - 1)
    q_sends = copies(lambda peer: qbuf.at[me], qbuf, qs_sem, qr_sem)
    x_sends = copies(lambda peer: xbuf.at[me], xbuf, xs_sem, xr_sem.at[me // 2])
    for send in q_sends + x_sends:
        send.start()

    def decode_gate_up(vals, mask, at):
        def body(i, carry):
            row = mask[pl.ds(i, 1), :].astype(F32) + F32(0.5)
            rows = vals[pl.ds(pl.multiple_of(i * 16, 16), 16), :]
            upper, lower = decode_rows(rows, row, 512)
            start = pl.multiple_of(i * 32, 32)
            wgu[pl.ds(start, 16), at : at + 512] = upper
            wgu[pl.ds(start + 16, 16), at : at + 512] = lower
            return carry

        lax.fori_loop(0, 64, body, 0)

    for load in loads[2:4]:
        load.wait()
    decode_gate_up(gv, gm, 0)
    for load in loads[4:]:
        load.wait()
    decode_gate_up(uv, um, 512)

    def decode_down(i, carry):
        for c in range(4):
            lanes = slice(c * 512, c * 512 + 512)
            row = dm[pl.ds(i, 1), lanes].astype(F32) + F32(0.5)
            rows = dv[pl.ds(pl.multiple_of(i * 16, 16), 16), lanes]
            upper, lower = decode_rows(rows, row, 512)
            start = pl.multiple_of(i * 32, 32)
            wd[pl.ds(start, 16), lanes] = upper
            wd[pl.ds(start + 16, 16), lanes] = lower
        return carry

    lax.fori_loop(0, 16, decode_down, 0)

    for index, (dx, dy) in enumerate(
        [(0, 0), (0, 1), (1, 0), (3, 0), (1, 1), (3, 1), (2, 0), (2, 1)]
    ):
        pair = lax.rem(mx + dx, nx) * (ny // 2) + lax.rem(my // 2 + dy, ny // 2)
        wait_bytes(xbuf.at[pl.ds(0, 1 if index == 0 else 2)], xr_sem.at[pair])
        block = jnp.concatenate([xbuf[2 * pair], xbuf[2 * pair + 1]], axis=1)
        if index == 5:
            wait_bytes(qbuf.at[0 : n - 1], qr_sem)
            total = jnp.sum(qbuf[:, 0, :], axis=0, keepdims=True)
            scale = lax.rsqrt(row_column(total, eye) / F32(n * 128) + F32(epsilon))
        depth = pl.ds(pl.multiple_of(pair * 256, 256), 256)
        if index < 7:
            for c in range(2):
                lanes = slice(c * 512, c * 512 + 512)
                product = jnp.dot(block, wgu[depth, lanes], preferred_element_type=F32)
                if index == 0:
                    acc[:, lanes] = product
                else:
                    acc[:, lanes] += product

    hidden = []
    for at in range(0, 512, 256):
        gate, up = [
            scale
            * (
                acc[:, lanes]
                + jnp.dot(block, wgu[depth, lanes], preferred_element_type=F32)
            )
            for lanes in (slice(at, at + 256), slice(512 + at, 768 + at))
        ]
        product = jax.nn.silu(gate) * up
        hidden += [
            jnp.take_along_axis(
                product[:, c : c + 128], order, axis=1, mode="promise_in_bounds"
            )
            for c in (0, 128)
        ]
    hidden = jnp.concatenate(hidden, axis=1).astype(BF16)

    p_sends = copies(lambda peer: part.at[peer], rbuf, ps_sem, pr_sem)

    def down(first, second):
        rows = [wd[:, pl.ds(pl.multiple_of(to * 128, 128), 128)] for to in (first, second)]
        return jnp.dot(hidden, jnp.concatenate(rows, axis=1), preferred_element_type=F32)

    owners = peers + [me]
    product = down(*owners[0:2])
    for at in range(0, n, 2):
        later = down(*owners[at + 2 : at + 4]) if at + 2 < n else None
        product = product.astype(BF16)
        part[owners[at]] = product[:, 0:128]
        part[owners[at + 1]] = product[:, 128:256]
        for send in p_sends[at : at + 2]:
            send.start()
        product = later

    wait_bytes(rbuf.at[0 : n - 1], pr_sem)
    summed = part[me].astype(F32)
    for peer in peers:
        summed += rbuf[peer].astype(F32)
    out = (x_ref[...].astype(F32) + summed).astype(BF16)
    out = out.astype(F32)
    so_ref[...] = out
    sbuf[me] = row_sums(out * out, eye)
    s_sends = copies(lambda peer: sbuf.at[me], sbuf, ss_sem, sr_sem)
    for send in s_sends:
        send.start()
    wait_bytes(sbuf.at[0 : n - 1], sr_sem)
    scale = lax.rsqrt(row_column(jnp.sum(sbuf[:, 0, :], axis=0, keepdims=True), eye) / F32(n * 128) + F32(epsilon))
    fn_ref[...] = scale * fgain_ref[...].astype(F32)
    for ref, sem in [(qbuf, qs_sem), (xbuf, xs_sem), (part, ps_sem), (sbuf, ss_sem)]:
        wait_bytes(ref.at[0 : n - 1], sem)


def solution(mesh):
    n = mesh.shape["mp"]
    vmem = pl.BlockSpec(memory_space=pltpu.VMEM)
    hbm = pl.BlockSpec(memory_space=pl.ANY)

    def step(stream, ngain, gv, gm, uv, um, dv, dm, fgain):
        block = pltpu.VMEM(stream.shape, F32)
        dma = pltpu.SemaphoreType.DMA
        out, factor = pl.pallas_call(
            functools.partial(kernel, n, 4),
            out_shape=(block, block),
            in_specs=[hbm] * 9,
            out_specs=(vmem, vmem),
            scratch_shapes=[
                pltpu.VMEM(stream.shape, BF16),
                pltpu.VMEM((1, 128), BF16),
                pltpu.VMEM((1, 128), BF16),
                pltpu.VMEM(gv.shape, BF16),
                pltpu.VMEM(uv.shape, BF16),
                pltpu.VMEM(dv.shape, BF16),
                pltpu.VMEM(gm.shape, jnp.int32),
                pltpu.VMEM(um.shape, jnp.int32),
                pltpu.VMEM(dm.shape, jnp.int32),
                pltpu.VMEM((2048, 1024), BF16),
                pltpu.VMEM((512, 2048), BF16),
                pltpu.VMEM((64, 1024), F32),
                pltpu.VMEM((n, 64, 128), BF16),
                pltpu.VMEM((n, 1, 128), F32),
                pltpu.VMEM((n, 64, 128), BF16),
                pltpu.VMEM((n, 64, 128), BF16),
                pltpu.VMEM((n, 1, 128), F32),
                dma((3,)),
                dma,
                dma,
                dma,
                dma((n // 2,)),
                dma,
                dma,
                dma,
                dma,
            ],
            compiler_params=pltpu.CompilerParams(collective_id=0, has_side_effects=True),
        )(stream, ngain.reshape(1, -1), fgain.reshape(1, -1), gv, gm, uv, um, dv, dm)
        return out.astype(BF16), (out * factor).astype(BF16)

    cols = P(None, "mp")
    return jax.shard_map(
        step,
        mesh=mesh,
        in_specs=(
            P("dp", "mp"),
            P("mp"),
            cols,
            cols,
            cols,
            cols,
            P("mp", None),
            P("mp", None),
            P("mp"),
        ),
        out_specs=(P("dp", "mp"), P("dp", "mp")),
        check_vma=False,
    )
```

```python
import functools

import jax
import jax.numpy as jnp
from jax import lax
from jax.experimental import pallas as pl
from jax.experimental.pallas import tpu as pltpu
from jax.sharding import PartitionSpec as P

MESH = pl.DeviceIdType.MESH
F32 = jnp.float32
BF16 = jnp.bfloat16
epsilon = 1e-05


def iota(shape, dim):
    return lax.broadcasted_iota(jnp.int32, shape, dim)


def sublanes(array, index):
    return jnp.take_along_axis(array, index, axis=0, mode="promise_in_bounds")


def decode_rows(vals, mask, width):
    group = iota((8, 128), 0)
    scale = jnp.zeros((8, 128), F32)
    for k in range(8):
        scale = jnp.where(group == k, F32(1.0 / 6 ** (k + 1)), scale)
    row = iota((16, 128), 0)
    odd = (row - row // 2 * 2).astype(F32).astype(BF16)
    second = odd > BF16(0.5)
    upper_top = BF16(3) - BF16(2) * odd
    lower_low = BF16(4.5) - odd
    lower_also = BF16(9) - BF16(7) * odd
    zero = jnp.zeros((16, 128), BF16)
    other = group + 1 - 2 * (group - group // 2 * 2)
    uppers, lowers = [], []
    for c in range(width // 128):
        lanes = slice(c * 128, c * 128 + 128)
        turn = jnp.broadcast_to(mask[:, lanes], (8, 128)) * scale
        digit = jnp.floor((turn - jnp.floor(turn)) * F32(6))
        digit = jnp.concatenate(
            [sublanes(digit, group // 2), sublanes(digit, group // 2 + 4)], axis=0
        ).astype(BF16)
        kept = vals[:, lanes]
        in_upper = digit < upper_top
        in_lower = (digit > lower_low) | (digit == lower_also)
        crossing = jnp.where(in_upper | in_lower, zero, kept).astype(F32)
        crossed = jnp.concatenate(
            [sublanes(crossing[:8], other), sublanes(crossing[8:], other)], axis=0
        ).astype(BF16)
        uppers.append(jnp.where(in_upper, kept, jnp.where(second, crossed, zero)))
        lowers.append(jnp.where(in_lower, kept, jnp.where(second, zero, crossed)))
    return jnp.concatenate(uppers, axis=1), jnp.concatenate(lowers, axis=1)


def column_order(shape):
    target = iota(shape, 1)
    q = target % 32
    return target // 32 * 32 + (q % 16) // 2 * 4 + q % 2 + q // 16 * 2


def row_sums(values, eye):
    sums = jnp.sum(values, axis=1, keepdims=True)
    return jnp.sum(jnp.where(eye, sums, F32(0)), axis=0, keepdims=True)


def row_column(row, eye):
    return jnp.sum(jnp.where(eye, row, F32(0)), axis=1, keepdims=True)


def kernel(
    n,
    ny,
    x_hbm,
    ngain_hbm,
    fgain_hbm,
    gv_hbm,
    gm_hbm,
    uv_hbm,
    um_hbm,
    dv_hbm,
    dm_hbm,
    so_ref,
    fn_ref,
    x_ref,
    ngain_ref,
    fgain_ref,
    gv,
    uv,
    dv,
    gm,
    um,
    dm,
    wgu,
    wd,
    acc,
    xbuf,
    qbuf,
    part,
    rbuf,
    sbuf,
    load_sem,
    qs_sem,
    qr_sem,
    xs_sem,
    xr_sem,
    ps_sem,
    pr_sem,
    ss_sem,
    sr_sem,
):
    me = lax.axis_index("mp")
    nx = n // ny
    mx, my = me // ny, me % ny
    loads = [
        pltpu.make_async_copy(src, dst, load_sem.at[i])
        for i, src, dst in [
            (0, x_hbm, x_ref),
            (0, ngain_hbm, ngain_ref),
            (1, gm_hbm, gm),
            (1, gv_hbm, gv),
            (2, um_hbm, um),
            (2, uv_hbm, uv),
            (3, dm_hbm, dm),
            (3, dv_hbm, dv),
            (3, fgain_hbm, fgain_ref),
        ]
    ]
    for load in loads[:2]:
        load.start()
    barrier = pltpu.get_barrier_semaphore()
    peers = [
        lax.rem(mx + dx, nx) * ny + lax.rem(my + dy, ny)
        for dx, dy in [
            (2, 2), (2, 1), (1, 2), (2, 3), (3, 2), (1, 1), (1, 3), (3, 1),
            (3, 3), (2, 0), (0, 2), (1, 0), (3, 0), (0, 1), (0, 3),
        ]
    ]
    for peer in peers:
        pl.semaphore_signal(barrier, inc=1, device_id={"mp": peer}, device_id_type=MESH)
    for load in loads[2:]:
        load.start()

    eye = iota((64, 128), 0) == iota((64, 128), 1)
    order = column_order((64, 128))
    for load in loads[:2]:
        load.wait()
    x = x_ref[...].astype(F32)
    gained = x * ngain_ref[...].astype(F32)
    gained = jnp.take_along_axis(gained, order, axis=1, mode="promise_in_bounds")
    xbuf[me] = gained.astype(BF16)
    qbuf[me] = row_sums(x * x, eye)

    def copies(src, dst, send, recv, low=0, high=n - 1):
        return [
            pltpu.make_async_remote_copy(
                src_ref=src(peer),
                dst_ref=dst.at[me],
                send_sem=send,
                recv_sem=recv,
                device_id={"mp": peer},
                device_id_type=MESH,
            )
            for peer in peers[low:high]
        ]

    def wait_bytes(ref, sem):
        pltpu.make_async_copy(ref, ref, sem).wait()

    pl.semaphore_wait(barrier, n - 1)
    q_sends = copies(lambda peer: qbuf.at[me], qbuf, qs_sem, qr_sem)
    x_sends = copies(lambda peer: xbuf.at[me], xbuf, xs_sem, xr_sem.at[me // 2])
    for send in q_sends + x_sends:
        send.start()

    def decode_gate_up(vals, mask, at):
        def body(i, carry):
            row = mask[pl.ds(i, 1), :].astype(F32) + F32(0.5)
            rows = vals[pl.ds(pl.multiple_of(i * 16, 16), 16), :]
            upper, lower = decode_rows(rows, row, 512)
            start = pl.multiple_of(i * 32, 32)
            wgu[pl.ds(start, 16), at : at + 512] = upper
            wgu[pl.ds(start + 16, 16), at : at + 512] = lower
            return carry

        lax.fori_loop(0, 64, body, 0)

    for load in loads[2:4]:
        load.wait()
    decode_gate_up(gv, gm, 0)
    for load in loads[4:6]:
        load.wait()
    decode_gate_up(uv, um, 512)
    for load in loads[6:]:
        load.wait()

    def decode_down(i, carry):
        for c in range(4):
            lanes = slice(c * 512, c * 512 + 512)
            row = dm[pl.ds(i, 1), lanes].astype(F32) + F32(0.5)
            rows = dv[pl.ds(pl.multiple_of(i * 16, 16), 16), lanes]
            upper, lower = decode_rows(rows, row, 512)
            start = pl.multiple_of(i * 32, 32)
            wd[pl.ds(start, 16), lanes] = upper
            wd[pl.ds(start + 16, 16), lanes] = lower
        return carry

    lax.fori_loop(0, 16, decode_down, 0)

    for index, (dx, dy) in enumerate(
        [(0, 0), (0, 1), (1, 0), (3, 0), (1, 1), (3, 1), (2, 0), (2, 1)]
    ):
        pair = lax.rem(mx + dx, nx) * (ny // 2) + lax.rem(my // 2 + dy, ny // 2)
        wait_bytes(xbuf.at[pl.ds(0, 1 if index == 0 else 2)], xr_sem.at[pair])
        block = jnp.concatenate([xbuf[2 * pair], xbuf[2 * pair + 1]], axis=1)
        if index == 5:
            wait_bytes(qbuf.at[0 : n - 1], qr_sem)
            total = jnp.sum(qbuf[:, 0, :], axis=0, keepdims=True)
            scale = lax.rsqrt(row_column(total, eye) / F32(n * 128) + F32(epsilon))
        depth = pl.ds(pl.multiple_of(pair * 256, 256), 256)
        for c in range(2):
            lanes = slice(c * 512, c * 512 + 512)
            product = jnp.dot(block, wgu[depth, lanes], preferred_element_type=F32)
            if index == 0:
                acc[:, lanes] = product
            else:
                acc[:, lanes] += product

    gate = acc[:, 0:512] * scale
    up = acc[:, 512:1024] * scale
    hidden = jax.nn.silu(gate) * up
    hidden = jnp.concatenate(
        [
            jnp.take_along_axis(
                hidden[:, c * 128 : c * 128 + 128], order, axis=1, mode="promise_in_bounds"
            )
            for c in range(4)
        ],
        axis=1,
    ).astype(BF16)

    p_sends = copies(lambda peer: part.at[peer], rbuf, ps_sem, pr_sem.at[0], 0, 9)
    p_sends += copies(lambda peer: part.at[peer], rbuf, ps_sem, pr_sem.at[1], 9)

    def down(first, second):
        rows = [wd[:, pl.ds(pl.multiple_of(to * 128, 128), 128)] for to in (first, second)]
        return jnp.dot(hidden, jnp.concatenate(rows, axis=1), preferred_element_type=F32)

    owners = peers + [me]
    product = down(*owners[0:2])
    for at in range(0, n, 2):
        later = down(*owners[at + 2 : at + 4]) if at + 2 < n else None
        product = product.astype(BF16)
        part[owners[at]] = product[:, 0:128]
        part[owners[at + 1]] = product[:, 128:256]
        for send in p_sends[at : at + 2]:
            send.start()
        product = later

    summed = x_ref[...].astype(F32) + part[me].astype(F32)
    for low, high in [(9, n - 1), (0, 9)]:
        wait_bytes(rbuf.at[0 : high - low], pr_sem.at[low // 9])
        for peer in peers[low:high]:
            summed += rbuf[peer].astype(F32)
    out = summed.astype(BF16)
    out = out.astype(F32)
    so_ref[...] = out
    sbuf[me] = row_sums(out * out, eye)
    s_sends = copies(lambda peer: sbuf.at[me], sbuf, ss_sem, sr_sem)
    for send in s_sends:
        send.start()
    wait_bytes(sbuf.at[0 : n - 1], sr_sem)
    scale = lax.rsqrt(row_column(jnp.sum(sbuf[:, 0, :], axis=0, keepdims=True), eye) / F32(n * 128) + F32(epsilon))
    fn_ref[...] = scale * fgain_ref[...].astype(F32)
    for ref, sem in [(qbuf, qs_sem), (xbuf, xs_sem), (part, ps_sem), (sbuf, ss_sem)]:
        wait_bytes(ref.at[0 : n - 1], sem)


def solution(mesh):
    n = mesh.shape["mp"]
    vmem = pl.BlockSpec(memory_space=pltpu.VMEM)
    hbm = pl.BlockSpec(memory_space=pl.ANY)

    def step(stream, ngain, gv, gm, uv, um, dv, dm, fgain):
        block = pltpu.VMEM(stream.shape, F32)
        dma = pltpu.SemaphoreType.DMA
        out, factor = pl.pallas_call(
            functools.partial(kernel, n, 4),
            out_shape=(block, block),
            in_specs=[hbm] * 9,
            out_specs=(vmem, vmem),
            scratch_shapes=[
                pltpu.VMEM(stream.shape, BF16),
                pltpu.VMEM((1, 128), BF16),
                pltpu.VMEM((1, 128), BF16),
                pltpu.VMEM(gv.shape, BF16),
                pltpu.VMEM(uv.shape, BF16),
                pltpu.VMEM(dv.shape, BF16),
                pltpu.VMEM(gm.shape, jnp.int32),
                pltpu.VMEM(um.shape, jnp.int32),
                pltpu.VMEM(dm.shape, jnp.int32),
                pltpu.VMEM((2048, 1024), BF16),
                pltpu.VMEM((512, 2048), BF16),
                pltpu.VMEM((64, 1024), F32),
                pltpu.VMEM((n, 64, 128), BF16),
                pltpu.VMEM((n, 1, 128), F32),
                pltpu.VMEM((n, 64, 128), BF16),
                pltpu.VMEM((n, 64, 128), BF16),
                pltpu.VMEM((n, 1, 128), F32),
                dma((4,)),
                dma,
                dma,
                dma,
                dma((n // 2,)),
                dma,
                dma((2,)),
                dma,
                dma,
            ],
            compiler_params=pltpu.CompilerParams(collective_id=0, has_side_effects=True),
        )(stream, ngain.reshape(1, -1), fgain.reshape(1, -1), gv, gm, uv, um, dv, dm)
        return out.astype(BF16), (out * factor).astype(BF16)

    cols = P(None, "mp")
    return jax.shard_map(
        step,
        mesh=mesh,
        in_specs=(
            P("dp", "mp"),
            P("mp"),
            cols,
            cols,
            cols,
            cols,
            P("mp", None),
            P("mp", None),
            P("mp"),
        ),
        out_specs=(P("dp", "mp"), P("dp", "mp")),
        check_vma=False,
    )
```
